32 devices in a mesh: dp: 4 (over y, core), ctx: 4 (over z), tp: 2 (over x).
Axes of the slice: x: 2, y: 2, z: 4, core: 2. Of those that a mesh axis runs over, the one named last changes fastest.
Arguments:
- query_rows: bfloat16 [2048, 128, 128], P(('dp', 'ctx'), 'tp'), parts along dimension 0, may hold values from -6 to 6
- key_rows: bfloat16 [2048, 8, 128], P(('dp', 'ctx'), 'tp'), parts along dimension 0, may hold values from -6 to 6
- value_rows: bfloat16 [2048, 8, 128], P(('dp', 'ctx'), 'tp'), parts along dimension 0, may hold values from -6 to 6
- out_grad: bfloat16 [2048, 128, 128], P(('dp', 'ctx'), 'tp'), parts along dimension 0, may hold values from -6 to 6
- softmax_delta: float32 [2, 64, 2048], P('tp', 'ctx', 'dp'), parts along dimension 2, may hold values from -4 to 4
- log_norm: float32 [2, 64, 2048], P('tp', 'ctx', 'dp'), parts along dimension 2
- doc_lengths: int32 [12], P('dp'), parts along dimension 0, may hold values from 1 to 384, as said below
Outputs:
- query_grad: bfloat16 [2048, 128, 128], P(('dp', 'ctx'), 'tp'), parts along dimension 0
- key_grad: bfloat16 [2048, 8, 128], P(('dp', 'ctx'), 'tp'), parts along dimension 0
- value_grad: bfloat16 [2048, 8, 128], P(('dp', 'ctx'), 'tp'), parts along dimension 0
The draws below stay inside these ranges and needn't reach their ends.
There are 4 independent parts, one for each index of `dp`. The reference program is written for one: setup_inputs(seed, part) draws one part's arguments, and reference() takes and returns one part's arrays. A program takes and returns all parts, laid end to end along the dimension named above; each array names one. Nothing has to cross between parts.
Inputs may be any that keep to these rules, and one draw needn't show every extreme that they name: `doc_lengths`: the 3 lengths sum to 512.
All inputs are finite; a program needn't handle non-finite values.
Results may differ from the reference program's by a relative error of at most 0.0056.
Values may be sent and summed in bfloat16 or wider, within the bound.
No kernel may reach another device: no remote copies, remote signals or barrier semaphores. Data moves between devices by JAX's collectives and lax.ppermute only.
A program may use at most 64 MiB of HBM per device.

```python
import jax
import jax.numpy as jnp
from jax import lax

Q_HEADS = 128
KV_HEADS = 8
HEAD_DIM = 128
DOC_MAX = 384
TILE = 128
ROW_BLOCK = 512
SEQ = 512
SHARE = 16
HEAD_GROUPS = 2
HEADS_TP = 64
HEADS_DEV = 16
PAIRS = 1
DOCS = 3


def pair_lengths(key):
    base_key = jax.random.fold_in(key, 7)
    first_key, pick_key = jax.random.split(base_key)
    lower_len = jax.random.randint(first_key, (PAIRS,), 1, DOC_MAX + 1)
    chosen = jax.random.randint(pick_key, (), 0, PAIRS)
    lower_len = jnp.where(jnp.arange(PAIRS) == chosen, DOC_MAX, lower_len)
    upper_len = DOC_MAX + 1 - lower_len
    pair_rows = jnp.stack([lower_len, upper_len], axis=1).reshape(2 * PAIRS).astype(jnp.int32)
    last_doc = jnp.full((1,), SEQ - PAIRS * (DOC_MAX + 1), jnp.int32)
    return jnp.concatenate([pair_rows, last_doc])


def draw_doc_lengths(key, part):
    return pair_lengths(key)


def draw_log_norm(key, part):
    lengths = pair_lengths(key)
    doc_ends = jnp.cumsum(lengths).astype(jnp.int32)
    doc_starts = doc_ends - lengths
    positions = jnp.arange(SEQ, dtype=jnp.int32)
    segment_ids = jnp.sum((positions[:, None] >= doc_ends[None, :]).astype(jnp.int32), axis=1)
    doc_begin = jnp.sum(jnp.where(jnp.arange(DOCS)[None, :] == segment_ids[:, None], doc_starts[None, :], 0), axis=1)
    visible = (positions - doc_begin + 1).astype(jnp.float32)
    jitter_key = jax.random.fold_in(key, 13)
    jitter = jax.random.uniform(jitter_key, (HEAD_GROUPS, HEADS_TP, SEQ), jnp.float32, -0.5, 0.5)
    return jnp.log(visible)[None, None, :] + 0.5 + jitter


def block_levels(rng, shape, cuts, least, largest):
    def one(position, blocks):
        draws = jax.random.uniform(jax.random.fold_in(jax.random.fold_in(rng, 6), position), (blocks,), jnp.float32, least / len(cuts), largest / len(cuts))
        return jnp.repeat(jnp.exp(draws), shape[position] // blocks).reshape((-1,) + (1,) * (len(shape) - position - 1))

    gain = one(*cuts[0])
    for cut in cuts[1:]:
        gain = gain * one(*cut)
    return gain


def centred(rng, shape, deviation, limit, pieces=(), kind=jnp.bfloat16):
    level = block_levels(rng, shape, pieces, -0.22, 0.18) if pieces else 1.0
    array = jax.random.normal(rng, shape, jnp.float32) * deviation * level
    return jnp.minimum(jnp.maximum(array, -limit), limit).astype(kind)


def setup_inputs(seed: int = 0, part: int = 0) -> dict:
    seeds = jax.random.split(jax.random.key(seed), 8)
    part_splits = jax.random.split(jax.random.fold_in(seeds[7], part), 8)
    return {
        "query_rows": centred(part_splits[0], (SEQ, Q_HEADS, HEAD_DIM), 1.0, 6.0, ((0, 4), (1, 2))),
        "key_rows": centred(part_splits[1], (SEQ, KV_HEADS, HEAD_DIM), 1.0, 6.0, ((0, 4), (1, 2))),
        "value_rows": centred(part_splits[2], (SEQ, KV_HEADS, HEAD_DIM), 1.0, 6.0, ((0, 4), (1, 2))),
        "out_grad": centred(part_splits[3], (SEQ, Q_HEADS, HEAD_DIM), 1.0, 6.0, ((0, 4), (1, 2))),
        "softmax_delta": centred(part_splits[4], (HEAD_GROUPS, HEADS_TP, SEQ), 1.0, 4.0, ((0, 2), (1, 4)), jnp.float32),
        "log_norm": draw_log_norm(jax.random.fold_in(jax.random.fold_in(seeds[7], part), 71), part),
        "doc_lengths": draw_doc_lengths(jax.random.fold_in(jax.random.fold_in(seeds[7], part), 71), part),
    }


def doc_segments(doc_lengths, seq_len):
    doc_ends = jnp.cumsum(doc_lengths).astype(jnp.int32)
    positions = jnp.arange(seq_len, dtype=jnp.int32)
    return jnp.sum((positions[:, None] >= doc_ends[None, :]).astype(jnp.int32), axis=1).astype(jnp.int32)


def pair_einsum(spec, left, right):
    return jnp.einsum(spec, left.astype(jnp.float32), right.astype(jnp.float32))


def tile_windows(rows, tiles, width):
    return jnp.stack([lax.slice_in_dim(rows, t * TILE, t * TILE + width, axis=0) for t in range(tiles)])


def spread_tiles(parts):
    tiles, width, head_dim = parts.shape
    total = jnp.zeros((ROW_BLOCK + DOC_MAX, head_dim), parts.dtype)
    for t in range(tiles):
        total = total.at[t * TILE:t * TILE + width].add(parts[t])
    return total


def block_grads(query_block, grad_block, delta_block, norm_block, key_span, value_span, row_seg, col_seg, first_row):
    tiles = ROW_BLOCK // TILE
    head_dim = query_block.shape[1]
    width = TILE + DOC_MAX
    scaling = head_dim ** -0.5
    query_tiles = query_block.reshape(tiles, TILE, head_dim)
    grad_tiles = grad_block.reshape(tiles, TILE, head_dim)
    key_win = tile_windows(key_span, tiles, width)
    value_win = tile_windows(value_span, tiles, width)
    seg_win = tile_windows(col_seg, tiles, width)
    row_pos = first_row + jnp.arange(ROW_BLOCK, dtype=jnp.int32).reshape(tiles, TILE)
    col_pos = (first_row - DOC_MAX + TILE * jnp.arange(tiles, dtype=jnp.int32)[:, None]
               + jnp.arange(width, dtype=jnp.int32)[None, :])
    allowed = ((row_seg.reshape(tiles, TILE)[:, :, None] == seg_win[:, None, :])
               & (row_pos[:, :, None] >= col_pos[:, None, :]) & (col_pos[:, None, :] >= 0))
    scores = pair_einsum("tid,tjd->tij", query_tiles, key_win) * scaling
    probs = jnp.where(allowed, jnp.exp(scores - norm_block.reshape(tiles, TILE)[:, :, None]), 0.0)
    probs_low = lax.optimization_barrier(probs.astype(jnp.bfloat16))
    value_part = pair_einsum("tij,tid->tjd", probs_low, grad_tiles)
    prob_grad = pair_einsum("tid,tjd->tij", grad_tiles, value_win)
    score_grad = lax.optimization_barrier(
        (probs * (prob_grad - delta_block.reshape(tiles, TILE)[:, :, None])).astype(jnp.bfloat16))
    query_part = pair_einsum("tij,tjd->tid", score_grad, key_win) * scaling
    key_part = pair_einsum("tij,tid->tjd", score_grad, query_tiles) * scaling
    return query_part.reshape(ROW_BLOCK, head_dim), spread_tiles(key_part), spread_tiles(value_part)


def head_pass(query_head, grad_head, delta_head, norm_head, key_pad, value_pad, segment_ids, segment_pad,
              key_acc, value_acc):
    seq_len, head_dim = query_head.shape
    span = ROW_BLOCK + DOC_MAX

    def one_block(block_no, carry):
        query_out, key_sum, value_sum = carry
        first_row = (block_no * ROW_BLOCK).astype(jnp.int32)
        query_part, key_part, value_part = block_grads(
            lax.dynamic_slice_in_dim(query_head, first_row, ROW_BLOCK, 0),
            lax.dynamic_slice_in_dim(grad_head, first_row, ROW_BLOCK, 0),
            lax.dynamic_slice_in_dim(delta_head, first_row, ROW_BLOCK, 0),
            lax.dynamic_slice_in_dim(norm_head, first_row, ROW_BLOCK, 0),
            lax.dynamic_slice_in_dim(key_pad, first_row, span, 0),
            lax.dynamic_slice_in_dim(value_pad, first_row, span, 0),
            lax.dynamic_slice_in_dim(segment_ids, first_row, ROW_BLOCK, 0),
            lax.dynamic_slice_in_dim(segment_pad, first_row, span, 0),
            first_row)
        query_out = lax.dynamic_update_slice_in_dim(query_out, query_part.astype(jnp.bfloat16), first_row, 0)
        key_sum = lax.dynamic_update_slice_in_dim(
            key_sum, lax.dynamic_slice_in_dim(key_sum, first_row, span, 0) + key_part, first_row, 0)
        value_sum = lax.dynamic_update_slice_in_dim(
            value_sum, lax.dynamic_slice_in_dim(value_sum, first_row, span, 0) + value_part, first_row, 0)
        return (query_out, key_sum, value_sum)

    start = (jnp.zeros((seq_len, head_dim), jnp.bfloat16), key_acc, value_acc)
    return lax.fori_loop(0, seq_len // ROW_BLOCK, one_block, start)


def reference(query_rows, key_rows, value_rows, out_grad, softmax_delta, log_norm, doc_lengths):
    segment_ids = doc_segments(doc_lengths, SEQ)
    segment_pad = jnp.concatenate([jnp.full((DOC_MAX,), -1, jnp.int32), segment_ids])
    deltas_flat = softmax_delta.reshape(Q_HEADS, SEQ)
    norms_flat = log_norm.reshape(Q_HEADS, SEQ)
    zero_rows = jnp.zeros((DOC_MAX, HEAD_DIM), jnp.bfloat16)

    def one_group(group_no):
        def one_head(carry, offset):
            head_no = (group_no * HEADS_DEV + offset).astype(jnp.int32)
            kv_no = (head_no // SHARE).astype(jnp.int32)
            query_head = lax.dynamic_index_in_dim(query_rows, head_no, 1, keepdims=False)
            grad_head = lax.dynamic_index_in_dim(out_grad, head_no, 1, keepdims=False)
            key_full = lax.dynamic_index_in_dim(key_rows, kv_no, 1, keepdims=False)
            value_full = lax.dynamic_index_in_dim(value_rows, kv_no, 1, keepdims=False)
            delta_head = lax.dynamic_index_in_dim(deltas_flat, head_no, 0, keepdims=False)
            norm_head = lax.dynamic_index_in_dim(norms_flat, head_no, 0, keepdims=False)
            key_pad = jnp.concatenate([zero_rows, key_full])
            value_pad = jnp.concatenate([zero_rows, value_full])
            query_out, key_sum, value_sum = head_pass(
                query_head, grad_head, delta_head, norm_head, key_pad, value_pad, segment_ids, segment_pad,
                carry[0], carry[1])
            return (key_sum, value_sum), query_out

        start_sums = (jnp.zeros((SEQ + DOC_MAX, HEAD_DIM), jnp.float32),
                      jnp.zeros((SEQ + DOC_MAX, HEAD_DIM), jnp.float32))
        sums, query_heads = lax.scan(one_head, start_sums, jnp.arange(HEADS_DEV, dtype=jnp.int32))
        return query_heads, sums[0][DOC_MAX:].astype(jnp.bfloat16), sums[1][DOC_MAX:].astype(jnp.bfloat16)

    query_groups, key_parts, value_parts = lax.map(one_group, jnp.arange(Q_HEADS // HEADS_DEV, dtype=jnp.int32))
    query_grad = query_groups.reshape(Q_HEADS, SEQ, HEAD_DIM).transpose(1, 0, 2)
    per_kv = SHARE // HEADS_DEV
    key_grad = key_parts.astype(jnp.float32).reshape(KV_HEADS, per_kv, SEQ, HEAD_DIM).sum(axis=1)
    value_grad = value_parts.astype(jnp.float32).reshape(KV_HEADS, per_kv, SEQ, HEAD_DIM).sum(axis=1)
    key_grad = key_grad.astype(jnp.bfloat16).transpose(1, 0, 2)
    value_grad = value_grad.astype(jnp.bfloat16).transpose(1, 0, 2)
    return (query_grad, key_grad, value_grad)
```

```python
import functools

import jax
import jax.numpy as jnp
from jax import lax
from jax.experimental import pallas as pl
from jax.experimental.pallas import tpu as pltpu
from jax.sharding import PartitionSpec as P

DOC_MAX = 384
LOG2E = 1.4426950408889634


def dot_nt(left, right):
    return lax.dot_general(left, right, (((1,), (1,)), ((), ())), preferred_element_type=jnp.float32)


def dot_nn(left, right):
    return lax.dot_general(left, right, (((1,), (0,)), ((), ())), preferred_element_type=jnp.float32)


def doc_starts(docs_ref, n_docs, row_tok):
    start = jnp.zeros_like(row_tok)
    end = jnp.int32(0)
    for d in range(n_docs):
        end = end + docs_ref[d]
        start = jnp.where(row_tok >= end, jnp.maximum(start, end), start)
    return start


def pair_kernel(shifts, n_docs, share, docs_ref, q_ref, g_ref, norm_ref, delta_ref, *refs):
    n = len(shifts)
    kv_refs, ds_refs, out_refs = refs[:n], refs[n : 2 * n], refs[2 * n :]
    tok, _, dim = q_ref.shape
    rows = tok * share
    keys = kv_refs[0].shape[2]
    scaling = dim ** (-0.5)
    chunk = lax.axis_index("ctx")
    q = q_ref[...].reshape(rows, dim)
    g = g_ref[...].reshape(rows, dim)
    row = lax.broadcasted_iota(jnp.int32, (1, rows), 1)
    row_tok = chunk * tok + row // share
    start = doc_starts(docs_ref, n_docs, row_tok)
    norm = norm_ref[0] * LOG2E
    delta = delta_ref[0]
    block = 512
    for s, kv_ref, ds_ref, out_ref in zip(shifts, kv_refs, ds_refs, out_refs):
        k = kv_ref[0, 0]
        v = kv_ref[1, 0]
        base = (chunk - s) * tok
        first = start - base
        last = row_tok - base
        dk = jnp.zeros((keys, dim), jnp.float32)
        dv = jnp.zeros((keys, dim), jnp.float32)
        for b in range(rows // block):
            cut = slice(b * block, (b + 1) * block)
            key_pos = lax.broadcasted_iota(jnp.int32, (keys, block), 0)
            ok = key_pos >= first[:, cut]
            if s == 0:
                ok = ok & (key_pos <= last[:, cut])
            scores = dot_nt(k, q[cut])
            probs = jnp.where(ok, jnp.exp2(scores * (scaling * LOG2E) - norm[:, cut]), 0.0)
            dv = dv + dot_nn(probs.astype(jnp.bfloat16), g[cut])
            prob_grad = dot_nt(v, g[cut])
            ds = (probs * (prob_grad - delta[:, cut])).astype(jnp.bfloat16)
            ds_ref[0, :, cut] = ds
            dk = dk + dot_nn(ds, q[cut])
        out_ref[0, 0] = (dk * scaling).astype(out_ref.dtype)
        out_ref[1, 0] = dv.astype(out_ref.dtype)


def pair_grads(shifts, docs, q, g, norm, delta, kvs, out_types):
    tok, heads, dim = q.shape
    kv_heads = kvs[0].shape[1]
    share = heads // kv_heads
    rows = tok * share
    keys = kvs[0].shape[2]
    n = len(shifts)
    q_spec = pl.BlockSpec((tok, share, dim), lambda i, d: (0, i, 0))
    row_spec = pl.BlockSpec((1, 1, rows), lambda i, d: (i, 0, 0))
    kv_spec = pl.BlockSpec((2, 1, keys, dim), lambda i, d: (0, i, 0, 0))
    ds_spec = pl.BlockSpec((1, keys, rows), lambda i, d: (i, 0, 0))
    out = pl.pallas_call(
        functools.partial(pair_kernel, shifts, docs.shape[0], share),
        grid_spec=pltpu.PrefetchScalarGridSpec(
            num_scalar_prefetch=1,
            grid=(kv_heads,),
            in_specs=[q_spec, q_spec, row_spec, row_spec] + [kv_spec] * n,
            out_specs=[ds_spec] * n + [kv_spec] * n,
        ),
        out_shape=[jax.ShapeDtypeStruct((kv_heads, keys, rows), jnp.bfloat16)] * n
        + [jax.ShapeDtypeStruct((2, kv_heads, keys, dim), t) for t in out_types],
        cost_estimate=pl.CostEstimate(
            flops=8 * n * kv_heads * keys * rows * dim,
            transcendentals=n * kv_heads * keys * rows,
            bytes_accessed=4 * tok * heads * dim + 2 * n * kv_heads * keys * rows,
        ),
        name="pair_" + "_".join(str(s) for s in shifts),
    )(docs, q, g, norm, delta, *kvs)
    return out[:n], out[n:]


def query_kernel(share, *refs):
    n = (len(refs) - 1) // 2
    ds_refs, kv_refs, out_ref = refs[:n], refs[n : 2 * n], refs[-1]
    tok, _, dim = out_ref.shape
    scaling = dim ** (-0.5)
    ds = jnp.concatenate([r[0] for r in ds_refs], axis=0)
    k = jnp.concatenate([r[0, 0] for r in kv_refs], axis=0)
    total = lax.dot_general(ds, k, (((0,), (0,)), ((), ())), preferred_element_type=jnp.float32)
    out_ref[...] = (total * scaling).astype(jnp.bfloat16).reshape(tok, share, dim)


def query_grads(ds_list, kvs, tok):
    kv_heads, keys, rows = ds_list[0].shape
    dim = kvs[0].shape[3]
    share = rows // tok
    n = len(kvs)
    return pl.pallas_call(
        functools.partial(query_kernel, share),
        grid=(kv_heads,),
        in_specs=[pl.BlockSpec((1, keys, rows), lambda i: (i, 0, 0))] * n
        + [pl.BlockSpec((1, 1, keys, dim), lambda i: (0, i, 0, 0))] * n,
        out_specs=pl.BlockSpec((tok, share, dim), lambda i: (0, i, 0)),
        out_shape=jax.ShapeDtypeStruct((tok, kv_heads * share, dim), jnp.bfloat16),
        cost_estimate=pl.CostEstimate(
            flops=2 * n * kv_heads * keys * rows * dim,
            transcendentals=0,
            bytes_accessed=2 * n * kv_heads * keys * rows,
        ),
        name="query_grads",
    )(*ds_list, *kvs)


def local(query_rows, key_rows, value_rows, out_grad, softmax_delta, log_norm, doc_lengths):
    groups = lax.axis_size("ctx")
    tok, heads, dim = query_rows.shape
    kv_heads = key_rows.shape[1]
    share = heads // kv_heads
    per_dev = heads // groups
    reach = min(groups - 1, -(-(DOC_MAX - 1) // tok))
    own = jnp.stack([key_rows, value_rows]).transpose(0, 2, 1, 3)

    def moved(x, s):
        pairs = [(i, i + s) for i in range(groups) if 0 <= i + s < groups]
        return lax.ppermute(x, "ctx", pairs)

    kvs = [own] + [moved(own, s) for s in range(1, reach + 1)]
    stats = jnp.stack([log_norm[0], softmax_delta[0]])
    stats = stats.reshape(2, per_dev, groups, tok).transpose(2, 0, 3, 1)
    stats = lax.all_to_all(stats, "ctx", split_axis=0, concat_axis=0, tiled=True)
    stats = stats.reshape(kv_heads, groups // kv_heads, 2, tok, per_dev)
    stats = stats.transpose(2, 0, 3, 1, 4).reshape(2, kv_heads, 1, tok * share)
    norm, delta = stats[0], stats[1]

    def grads(shifts, types):
        return pair_grads(
            shifts, doc_lengths, query_rows, out_grad, norm, delta, [kvs[s] for s in shifts], types
        )

    ds_list, back = grads((0, 1), (jnp.float32, jnp.bfloat16))
    total = back[0]
    terms = [moved(back[1], -1)]
    for s in range(2, reach + 1):
        ds, part = grads((s,), (jnp.bfloat16,))
        ds_list = ds_list + ds
        terms.append(moved(part[0], -s))
    query_grad = query_grads(ds_list, kvs, tok)
    for term in terms:
        total = total + term.astype(jnp.float32)
    total = total.astype(jnp.bfloat16).transpose(0, 2, 1, 3)
    return (query_grad, total[0], total[1])


def solution(mesh):
    rows = P(("dp", "ctx"), "tp", None)
    stats = P("tp", "ctx", "dp")
    return jax.shard_map(
        local,
        mesh=mesh,
        in_specs=(rows, rows, rows, rows, stats, stats, P("dp")),
        out_specs=(rows, rows, rows),
        check_vma=False,
    )
```

```python
import functools

import jax
import jax.numpy as jnp
from jax import lax
from jax.experimental import pallas as pl
from jax.experimental.pallas import tpu as pltpu
from jax.sharding import PartitionSpec as P


DOC_MAX = 384
LOG2E = 1.4426950408889634
MIB = 1024 * 1024
VMEM = pl.BlockSpec(memory_space=pltpu.VMEM)
HBM = pl.BlockSpec(memory_space=pltpu.HBM)


def dot_nt(left, right):
    return lax.dot_general(left, right, (((1,), (1,)), ((), ())), preferred_element_type=jnp.float32)


def dot_nn(left, right):
    return lax.dot_general(left, right, (((1,), (0,)), ((), ())), preferred_element_type=jnp.float32)


def doc_start(docs_ref, token):
    start = jnp.zeros_like(token)
    end = jnp.int32(0)
    for d in range(docs_ref.shape[0]):
        end = end + docs_ref[d]
        start = jnp.where(token >= end, end, start)
    return start


def row_tokens(rows, share, first):
    return first + lax.broadcasted_iota(jnp.int32, (1, rows), 1) // share


def spread_stats(share, in_ref, out_ref):
    kv_heads, _, _, tok = in_ref.shape
    rows = tok * share
    at = lax.broadcasted_iota(jnp.int32, (tok, rows), 1) // share
    spread = (at == lax.broadcasted_iota(jnp.int32, (tok, rows), 0)).astype(jnp.float32)
    spread = spread.astype(jnp.bfloat16)
    head = lax.broadcasted_iota(jnp.int32, (share, rows), 0)
    own = lax.broadcasted_iota(jnp.int32, (share, rows), 1) % share == head
    for i in range(kv_heads):
        x = in_ref[i].reshape(2 * share, tok)
        high = x.astype(jnp.bfloat16)
        rest = x - high.astype(jnp.float32)
        mid = rest.astype(jnp.bfloat16)
        low = (rest - mid.astype(jnp.float32)).astype(jnp.bfloat16)
        y = dot_nn(high, spread) + dot_nn(mid, spread) + dot_nn(low, spread)
        out_ref[i, 0:1] = jnp.sum(jnp.where(own, y[:share], 0.0), axis=0, keepdims=True) * LOG2E
        out_ref[i, 1:2] = jnp.sum(jnp.where(own, y[share:], 0.0), axis=0, keepdims=True)


def tile_grads(k, v, q, g, norm, delta, ok):
    scores = dot_nt(k, q)
    probs = jnp.exp2(scores * (q.shape[1] ** (-0.5) * LOG2E) - norm)
    if ok is not None:
        probs = jnp.where(ok, probs, 0.0)
    ds = (probs * (dot_nt(v, g) - delta)).astype(jnp.bfloat16)
    return ds, dot_nn(ds, q), dot_nn(probs.astype(jnp.bfloat16), g)


def head_rows(ref, i, share, first, count):
    block = ref[pl.ds(first, count), pl.ds(pl.multiple_of(i * share, share), share), :]
    return block.reshape(count * share, ref.shape[2])


def past_kernel(shift, share, start_ref, q_ref, g_ref, stats_ref, kv_ref, ds_ref, out_ref, acc_ref, ready):
    tok, _, dim = q_ref.shape
    _, kv_heads, keys, _ = kv_ref.shape
    scaling = dim ** (-0.5)
    base = (lax.axis_index("ctx") - shift) * keys
    none = (base < 0) | (jnp.min(start_ref[...]) >= base + keys)
    full = jnp.logical_not(none) & (jnp.max(start_ref[...]) <= base)

    @pl.when(full)
    def _():
        for i in range(kv_heads):
            ready(i)
            q = head_rows(q_ref, i, share, 0, tok)
            g = head_rows(g_ref, i, share, 0, tok)
            ds, dk, dv = tile_grads(
                kv_ref[0, i], kv_ref[1, i], q, g, stats_ref[i, 0:1], stats_ref[i, 1:2], None
            )
            ds_ref[i] = ds
            out_ref[0, i] = (dk * scaling).astype(jnp.bfloat16)
            out_ref[1, i] = dv.astype(jnp.bfloat16)

    @pl.when(jnp.logical_not(full))
    def _():
        for i in range(kv_heads):
            ready(i)

    @pl.when(none)
    def _():
        ds_ref[...] = jnp.zeros_like(ds_ref)
        out_ref[...] = jnp.zeros_like(out_ref)

    @pl.when(jnp.logical_not(none | full))
    def _():
        step = 32

        def one_head(i, _):
            acc_ref[...] = jnp.zeros_like(acc_ref)
            for b in range(tok // step):
                cut = slice(b * step * share, (b + 1) * step * share)
                start = start_ref[:, cut]
                reached = jnp.min(start) < base + keys

                @pl.when(reached)
                def _():
                    q = head_rows(q_ref, i, share, b * step, step)
                    g = head_rows(g_ref, i, share, b * step, step)
                    key = base + lax.broadcasted_iota(jnp.int32, (keys, step * share), 0)
                    ds, dk, dv = tile_grads(
                        kv_ref[0, i],
                        kv_ref[1, i],
                        q,
                        g,
                        stats_ref[i, 0:1, cut],
                        stats_ref[i, 1:2, cut],
                        key >= start,
                    )
                    ds_ref[i, :, cut] = ds
                    acc_ref[0] += dk
                    acc_ref[1] += dv

                @pl.when(jnp.logical_not(reached))
                def _():
                    ds_ref[i, :, cut] = jnp.zeros((keys, step * share), jnp.bfloat16)

            out_ref[0, i] = (acc_ref[0] * scaling).astype(jnp.bfloat16)
            out_ref[1, i] = acc_ref[1].astype(jnp.bfloat16)
            return 0

        lax.fori_loop(0, kv_heads, one_head, 0)


def first_past_kernel(share, docs_hbm, q_hbm, g_hbm, raw_ref, kv_ref, *refs):
    ds_ref, out_ref, q_ref, g_ref, stats_ref, start_ref, acc_ref, docs_ref, docs_sem, q_sem, g_sem = refs
    tok = q_ref.shape[0]

    def copies(i):
        heads = pl.ds(i * share, share)
        return (
            pltpu.make_async_copy(q_hbm.at[:, heads, :], q_ref.at[:, heads, :], q_sem.at[i]),
            pltpu.make_async_copy(g_hbm.at[:, heads, :], g_ref.at[:, heads, :], g_sem.at[i]),
        )

    def ready(i):
        for copy in copies(i):
            copy.wait()

    docs_copy = pltpu.make_async_copy(docs_hbm, docs_ref, docs_sem)
    docs_copy.start()
    for i in range(kv_ref.shape[1]):
        for copy in copies(i):
            copy.start()
    spread_stats(share, raw_ref, stats_ref)
    docs_copy.wait()
    token = row_tokens(tok * share, share, lax.axis_index("ctx") * tok)
    start_ref[...] = doc_start(docs_ref, token)
    past_kernel(1, share, start_ref, q_ref, g_ref, stats_ref, kv_ref, ds_ref, out_ref, acc_ref, ready)


def next_past_kernel(shift, share, *refs):
    past_kernel(shift, share, *refs, lambda i: None)


def past_cost(kv, rows):
    _, kv_heads, keys, dim = kv.shape
    return pl.CostEstimate(
        flops=8 * kv_heads * keys * rows * dim,
        transcendentals=kv_heads * keys * rows,
        bytes_accessed=4 * kv_heads * rows * dim,
    )


def first_past(share, docs, q, g, raw, kv):
    _, kv_heads, keys, dim = kv.shape
    rows = q.shape[0] * share
    return pl.pallas_call(
        functools.partial(first_past_kernel, share),
        in_specs=[HBM, HBM, HBM, VMEM, VMEM],
        out_specs=[VMEM] * 6,
        out_shape=[
            jax.ShapeDtypeStruct((kv_heads, keys, rows), jnp.bfloat16),
            jax.ShapeDtypeStruct(kv.shape, jnp.bfloat16),
            jax.ShapeDtypeStruct(q.shape, q.dtype),
            jax.ShapeDtypeStruct(g.shape, g.dtype),
            jax.ShapeDtypeStruct((kv_heads, 2, rows), jnp.float32),
            jax.ShapeDtypeStruct((1, rows), jnp.int32),
        ],
        scratch_shapes=[
            pltpu.VMEM((2, keys, dim), jnp.float32),
            pltpu.SMEM(docs.shape, jnp.int32),
            pltpu.SemaphoreType.DMA,
            pltpu.SemaphoreType.DMA((kv_heads,)),
            pltpu.SemaphoreType.DMA((kv_heads,)),
        ],
        compiler_params=pltpu.CompilerParams(vmem_limit_bytes=47 * MIB),
        cost_estimate=past_cost(kv, rows),
        name="past_1",
    )(docs, q, g, raw, kv)


def next_past(shift, share, start, q, g, stats, kv):
    _, kv_heads, keys, dim = kv.shape
    rows = stats.shape[2]
    return pl.pallas_call(
        functools.partial(next_past_kernel, shift, share),
        in_specs=[VMEM] * 5,
        out_specs=[VMEM, VMEM],
        out_shape=[
            jax.ShapeDtypeStruct((kv_heads, keys, rows), jnp.bfloat16),
            jax.ShapeDtypeStruct(kv.shape, jnp.bfloat16),
        ],
        scratch_shapes=[pltpu.VMEM((2, keys, dim), jnp.float32)],
        compiler_params=pltpu.CompilerParams(vmem_limit_bytes=24 * MIB),
        cost_estimate=past_cost(kv, rows),
    )(start, q, g, stats, kv)


def last_kernel(share, start_ref, q_ref, g_ref, stats_ref, kv_ref, *refs):
    n = (len(refs) - 2) // 2
    past_kv, past_ds, (dq_ref, out_ref) = refs[:n], refs[n : 2 * n], refs[2 * n :]
    tok, _, dim = q_ref.shape
    _, kv_heads, keys, _ = kv_ref.shape
    rows = tok * share
    scaling = dim ** (-0.5)
    first = lax.axis_index("ctx") * tok
    key = first + lax.broadcasted_iota(jnp.int32, (keys, rows), 0)
    ok = (key >= start_ref[...]) & (key <= row_tokens(rows, share, first))
    for i in range(kv_heads):
        k = kv_ref[0, i]
        q = head_rows(q_ref, i, share, 0, tok)
        g = head_rows(g_ref, i, share, 0, tok)
        ds, dk, dv = tile_grads(k, kv_ref[1, i], q, g, stats_ref[i, 0:1], stats_ref[i, 1:2], ok)
        out_ref[0, i] = dk * scaling
        out_ref[1, i] = dv
        ks = jnp.concatenate([k] + [r[0, i] for r in past_kv], axis=0)
        ds = jnp.concatenate([ds] + [r[i] for r in past_ds], axis=0)
        dq = dot_nn(ks.T, ds) * scaling
        dq_ref[:, i * share : (i + 1) * share, :] = dq.T.astype(jnp.bfloat16).reshape(tok, share, dim)


def last_grads(share, start, q, g, stats, kvs, ds_list):
    _, kv_heads, keys, dim = kvs[0].shape
    rows = stats.shape[2]
    n = len(kvs)
    return pl.pallas_call(
        functools.partial(last_kernel, share),
        in_specs=[VMEM] * (4 + n + len(ds_list)),
        out_specs=[VMEM, VMEM],
        out_shape=[
            jax.ShapeDtypeStruct(q.shape, jnp.bfloat16),
            jax.ShapeDtypeStruct(kvs[0].shape, jnp.float32),
        ],
        compiler_params=pltpu.CompilerParams(vmem_limit_bytes=24 * MIB),
        cost_estimate=pl.CostEstimate(
            flops=(8 + 2 * n) * kv_heads * keys * rows * dim,
            transcendentals=kv_heads * keys * rows,
            bytes_accessed=4 * kv_heads * rows * dim,
        ),
        name="last",
    )(start, q, g, stats, *kvs, *ds_list)


def local(query_rows, key_rows, value_rows, out_grad, softmax_delta, log_norm, doc_lengths):
    groups = lax.axis_size("ctx")
    tok, heads, _ = query_rows.shape
    kv_heads = key_rows.shape[1]
    share = heads // kv_heads
    per_dev = heads // groups
    reach = min(groups - 1, -(-(DOC_MAX - 1) // tok))

    def moved(x, s):
        pairs = [(i, i + s) for i in range(groups) if 0 <= i + s < groups]
        return lax.ppermute(x, "ctx", pairs)

    kvs = [jnp.stack([key_rows, value_rows]).transpose(0, 2, 1, 3)]
    for _ in range(1, reach + 1):
        kvs.append(moved(kvs[-1], 1))
    raw = jnp.stack([log_norm[0], softmax_delta[0]])
    raw = raw.reshape(2, per_dev, groups, tok).transpose(2, 0, 1, 3)
    raw = lax.all_to_all(raw, "ctx", split_axis=0, concat_axis=0, tiled=True)
    raw = raw.reshape(kv_heads, groups // kv_heads, 2, per_dev, tok)
    raw = raw.transpose(0, 2, 1, 3, 4).reshape(kv_heads, 2, share, tok)
    ds, part, q, g, stats, start = first_past(share, doc_lengths, query_rows, out_grad, raw, kvs[1])
    terms = [moved(part, -1)]
    ds_list = [ds]
    for s in range(2, reach + 1):
        ds, part = next_past(s, share, start, q, g, stats, kvs[s])
        ds_list.append(ds)
        terms.append(moved(part, -s))
    query_grad, total = last_grads(share, start, q, g, stats, kvs, ds_list)
    for term in terms:
        total = total + term.astype(jnp.float32)
    total = total.astype(jnp.bfloat16).transpose(0, 2, 1, 3)
    return (query_grad, total[0], total[1])


def solution(mesh):
    rows = P(("dp", "ctx"), "tp", None)
    stats = P("tp", "ctx", "dp")
    return jax.shard_map(
        local,
        mesh=mesh,
        in_specs=(rows, rows, rows, rows, stats, stats, P("dp")),
        out_specs=(rows, rows, rows),
        check_vma=False,
    )
```

```python
import functools

import jax
import jax.numpy as jnp
from jax import lax
from jax.experimental import pallas as pl
from jax.experimental.pallas import tpu as pltpu
from jax.sharding import PartitionSpec as P


DOC_MAX = 384
LOG2E = 1.4426950408889634
MIB = 1024 * 1024
VMEM = pl.BlockSpec(memory_space=pltpu.VMEM)
HBM = pl.BlockSpec(memory_space=pltpu.HBM)


def dot_nt(left, right):
    return lax.dot_general(left, right, (((1,), (1,)), ((), ())), preferred_element_type=jnp.float32)


def dot_nn(left, right):
    return lax.dot_general(left, right, (((1,), (0,)), ((), ())), preferred_element_type=jnp.float32)


def doc_start(docs_ref, token):
    start = jnp.zeros_like(token)
    end = jnp.int32(0)
    for d in range(docs_ref.shape[0]):
        end = end + docs_ref[d]
        start = jnp.where(token >= end, end, start)
    return start


def row_tokens(rows, share, first):
    return first + lax.broadcasted_iota(jnp.int32, (1, rows), 1) // share


def spread_stats(share, in_ref, out_ref):
    kv_heads, _, _, tok = in_ref.shape
    rows = tok * share
    x = in_ref[...].reshape(kv_heads * 2 * share, tok)
    high = x.astype(jnp.bfloat16)
    rest = x - high.astype(jnp.float32)
    mid = rest.astype(jnp.bfloat16)
    low = (rest - mid.astype(jnp.float32)).astype(jnp.bfloat16)
    at = lax.broadcasted_iota(jnp.int32, (tok, rows), 1) // share
    spread = (at == lax.broadcasted_iota(jnp.int32, (tok, rows), 0)).astype(jnp.float32)
    spread = spread.astype(jnp.bfloat16)
    parts = jnp.concatenate([high, mid, low], axis=1)
    y = dot_nn(parts, jnp.concatenate([spread] * 3, axis=0))
    own = lax.broadcasted_iota(jnp.int32, (share, rows), 1) % share
    own = own == lax.broadcasted_iota(jnp.int32, (share, rows), 0)
    for i in range(kv_heads):
        for j, factor in ((0, LOG2E), (1, 1.0)):
            first = (2 * i + j) * share
            row = jnp.sum(jnp.where(own, y[first : first + share], 0.0), axis=0, keepdims=True)
            out_ref[i, j : j + 1] = row * factor


def tile_grads(k, v, q, g, norm, delta, ok):
    scores = dot_nt(k, q)
    probs = jnp.exp2(scores * (q.shape[1] ** (-0.5) * LOG2E) - norm)
    if ok is not None:
        probs = jnp.where(ok, probs, 0.0)
    ds = (probs * (dot_nt(v, g) - delta)).astype(jnp.bfloat16)
    return ds, dot_nn(ds, q), dot_nn(probs.astype(jnp.bfloat16), g)


def head_rows(ref, i, share, first, count):
    block = ref[pl.ds(first, count), pl.ds(pl.multiple_of(i * share, share), share), :]
    return block.reshape(count * share, ref.shape[2])


def past_kernel(shift, share, start_ref, q_ref, g_ref, stats_ref, kv_ref, ds_ref, out_ref, acc_ref, ready):
    tok, _, dim = q_ref.shape
    _, kv_heads, keys, _ = kv_ref.shape
    scaling = dim ** (-0.5)
    base = (lax.axis_index("ctx") - shift) * keys
    none = (base < 0) | (jnp.min(start_ref[...]) >= base + keys)
    full = jnp.logical_not(none) & (jnp.max(start_ref[...]) <= base)

    @pl.when(full)
    def _():
        for i in range(kv_heads):
            ready(i)
            q = head_rows(q_ref, i, share, 0, tok)
            g = head_rows(g_ref, i, share, 0, tok)
            ds, dk, dv = tile_grads(
                kv_ref[0, i], kv_ref[1, i], q, g, stats_ref[i, 0:1], stats_ref[i, 1:2], None
            )
            ds_ref[i] = ds
            out_ref[0, i] = (dk * scaling).astype(jnp.bfloat16)
            out_ref[1, i] = dv.astype(jnp.bfloat16)

    @pl.when(jnp.logical_not(full))
    def _():
        for i in range(kv_heads):
            ready(i)

    @pl.when(none)
    def _():
        ds_ref[...] = jnp.zeros_like(ds_ref)
        out_ref[...] = jnp.zeros_like(out_ref)

    @pl.when(jnp.logical_not(none | full))
    def _():
        step = 32

        def one_head(i, _):
            acc_ref[...] = jnp.zeros_like(acc_ref)
            for b in range(tok // step):
                cut = slice(b * step * share, (b + 1) * step * share)
                start = start_ref[:, cut]
                reached = jnp.min(start) < base + keys

                @pl.when(reached)
                def _():
                    q = head_rows(q_ref, i, share, b * step, step)
                    g = head_rows(g_ref, i, share, b * step, step)
                    key = base + lax.broadcasted_iota(jnp.int32, (keys, step * share), 0)
                    ds, dk, dv = tile_grads(
                        kv_ref[0, i],
                        kv_ref[1, i],
                        q,
                        g,
                        stats_ref[i, 0:1, cut],
                        stats_ref[i, 1:2, cut],
                        key >= start,
                    )
                    ds_ref[i, :, cut] = ds
                    acc_ref[0] += dk
                    acc_ref[1] += dv

                @pl.when(jnp.logical_not(reached))
                def _():
                    ds_ref[i, :, cut] = jnp.zeros((keys, step * share), jnp.bfloat16)

            out_ref[0, i] = (acc_ref[0] * scaling).astype(jnp.bfloat16)
            out_ref[1, i] = acc_ref[1].astype(jnp.bfloat16)
            return 0

        lax.fori_loop(0, kv_heads, one_head, 0)


def first_past_kernel(share, docs_hbm, q_hbm, g_hbm, raw_ref, kv_ref, *refs):
    ds_ref, out_ref, q_ref, g_ref, stats_ref, start_ref, acc_ref, docs_ref, docs_sem, q_sem, g_sem = refs
    tok = q_ref.shape[0]

    def copies(i):
        heads = pl.ds(i * share, share)
        return (
            pltpu.make_async_copy(q_hbm.at[:, heads, :], q_ref.at[:, heads, :], q_sem.at[i]),
            pltpu.make_async_copy(g_hbm.at[:, heads, :], g_ref.at[:, heads, :], g_sem.at[i]),
        )

    def ready(i):
        for copy in copies(i):
            copy.wait()

    docs_copy = pltpu.make_async_copy(docs_hbm, docs_ref, docs_sem)
    docs_copy.start()
    for i in range(kv_ref.shape[1]):
        for copy in copies(i):
            copy.start()
    spread_stats(share, raw_ref, stats_ref)
    docs_copy.wait()
    token = row_tokens(tok * share, share, lax.axis_index("ctx") * tok)
    start_ref[...] = doc_start(docs_ref, token)
    past_kernel(1, share, start_ref, q_ref, g_ref, stats_ref, kv_ref, ds_ref, out_ref, acc_ref, ready)


def next_past_kernel(shift, share, *refs):
    past_kernel(shift, share, *refs, lambda i: None)


def past_cost(kv, rows):
    _, kv_heads, keys, dim = kv.shape
    return pl.CostEstimate(
        flops=8 * kv_heads * keys * rows * dim,
        transcendentals=kv_heads * keys * rows,
        bytes_accessed=4 * kv_heads * rows * dim,
    )


def first_past(share, docs, q, g, raw, kv):
    _, kv_heads, keys, dim = kv.shape
    rows = q.shape[0] * share
    return pl.pallas_call(
        functools.partial(first_past_kernel, share),
        in_specs=[HBM, HBM, HBM, VMEM, VMEM],
        out_specs=[VMEM] * 6,
        out_shape=[
            jax.ShapeDtypeStruct((kv_heads, keys, rows), jnp.bfloat16),
            jax.ShapeDtypeStruct(kv.shape, jnp.bfloat16),
            jax.ShapeDtypeStruct(q.shape, q.dtype),
            jax.ShapeDtypeStruct(g.shape, g.dtype),
            jax.ShapeDtypeStruct((kv_heads, 2, rows), jnp.float32),
            jax.ShapeDtypeStruct((1, rows), jnp.int32),
        ],
        scratch_shapes=[
            pltpu.VMEM((2, keys, dim), jnp.float32),
            pltpu.SMEM(docs.shape, jnp.int32),
            pltpu.SemaphoreType.DMA,
            pltpu.SemaphoreType.DMA((kv_heads,)),
            pltpu.SemaphoreType.DMA((kv_heads,)),
        ],
        compiler_params=pltpu.CompilerParams(vmem_limit_bytes=47 * MIB),
        cost_estimate=past_cost(kv, rows),
        name="past_1",
    )(docs, q, g, raw, kv)


def next_past(shift, share, start, q, g, stats, kv):
    _, kv_heads, keys, dim = kv.shape
    rows = stats.shape[2]
    return pl.pallas_call(
        functools.partial(next_past_kernel, shift, share),
        in_specs=[VMEM] * 5,
        out_specs=[VMEM, VMEM],
        out_shape=[
            jax.ShapeDtypeStruct((kv_heads, keys, rows), jnp.bfloat16),
            jax.ShapeDtypeStruct(kv.shape, jnp.bfloat16),
        ],
        scratch_shapes=[pltpu.VMEM((2, keys, dim), jnp.float32)],
        compiler_params=pltpu.CompilerParams(vmem_limit_bytes=24 * MIB),
        cost_estimate=past_cost(kv, rows),
    )(start, q, g, stats, kv)


def last_kernel(share, start_ref, q_ref, g_ref, stats_ref, kv_ref, *refs):
    n = (len(refs) - 2) // 2
    past_kv, past_ds, (dq_ref, out_ref) = refs[:n], refs[n : 2 * n], refs[2 * n :]
    tok, _, dim = q_ref.shape
    _, kv_heads, keys, _ = kv_ref.shape
    rows = tok * share
    scaling = dim ** (-0.5)
    first = lax.axis_index("ctx") * tok
    key = first + lax.broadcasted_iota(jnp.int32, (keys, rows), 0)
    ok = (key >= start_ref[...]) & (key <= row_tokens(rows, share, first))
    for i in range(kv_heads):
        k = kv_ref[0, i]
        q = head_rows(q_ref, i, share, 0, tok)
        g = head_rows(g_ref, i, share, 0, tok)
        ds, dk, dv = tile_grads(k, kv_ref[1, i], q, g, stats_ref[i, 0:1], stats_ref[i, 1:2], ok)
        out_ref[0, i] = dk * scaling
        out_ref[1, i] = dv
        ks = jnp.concatenate([k] + [r[0, i] for r in past_kv], axis=0)
        ds = jnp.concatenate([ds] + [r[i] for r in past_ds], axis=0)
        dq = dot_nn(ks.T, ds) * scaling
        dq_ref[:, i * share : (i + 1) * share, :] = dq.T.astype(jnp.bfloat16).reshape(tok, share, dim)


def last_grads(share, start, q, g, stats, kvs, ds_list):
    _, kv_heads, keys, dim = kvs[0].shape
    rows = stats.shape[2]
    n = len(kvs)
    return pl.pallas_call(
        functools.partial(last_kernel, share),
        in_specs=[VMEM] * (4 + n + len(ds_list)),
        out_specs=[VMEM, VMEM],
        out_shape=[
            jax.ShapeDtypeStruct(q.shape, jnp.bfloat16),
            jax.ShapeDtypeStruct(kvs[0].shape, jnp.float32),
        ],
        compiler_params=pltpu.CompilerParams(vmem_limit_bytes=24 * MIB),
        cost_estimate=pl.CostEstimate(
            flops=(8 + 2 * n) * kv_heads * keys * rows * dim,
            transcendentals=kv_heads * keys * rows,
            bytes_accessed=4 * kv_heads * rows * dim,
        ),
        name="last",
    )(start, q, g, stats, *kvs, *ds_list)


def sum_kernel(*refs):
    own_ref, terms, (key_ref, value_ref) = refs[0], refs[1:-2], refs[-2:]
    for j, ref in enumerate((key_ref, value_ref)):
        total = own_ref[j]
        for term in terms:
            total = total + term[j].astype(jnp.float32)
        ref[...] = jnp.swapaxes(total, 0, 1).astype(jnp.bfloat16)


def sum_terms(own, terms):
    _, kv_heads, keys, dim = own.shape
    return pl.pallas_call(
        sum_kernel,
        in_specs=[VMEM] * (1 + len(terms)),
        out_shape=[jax.ShapeDtypeStruct((keys, kv_heads, dim), jnp.bfloat16)] * 2,
        compiler_params=pltpu.CompilerParams(vmem_limit_bytes=24 * MIB),
        name="sum",
    )(own, *terms)


def local(query_rows, key_rows, value_rows, out_grad, softmax_delta, log_norm, doc_lengths):
    groups = lax.axis_size("ctx")
    tok, heads, _ = query_rows.shape
    kv_heads = key_rows.shape[1]
    share = heads // kv_heads
    per_dev = heads // groups
    reach = min(groups - 1, -(-(DOC_MAX - 1) // tok))

    def moved(x, s):
        pairs = [(i, i + s) for i in range(groups) if 0 <= i + s < groups]
        return lax.ppermute(x, "ctx", pairs)

    kvs = [jnp.stack([key_rows, value_rows]).transpose(0, 2, 1, 3)]
    for _ in range(1, reach + 1):
        kvs.append(moved(kvs[-1], 1))
    raw = jnp.stack([log_norm[0], softmax_delta[0]])
    raw = raw.reshape(2, per_dev, groups, tok).transpose(2, 0, 1, 3)
    raw = lax.all_to_all(raw, "ctx", split_axis=0, concat_axis=0, tiled=True)
    raw = raw.reshape(kv_heads, groups // kv_heads, 2, per_dev, tok)
    raw = raw.transpose(0, 2, 1, 3, 4).reshape(kv_heads, 2, share, tok)
    docs = jnp.maximum(doc_lengths, 1)
    ds, part, q, g, stats, start = first_past(share, docs, query_rows, out_grad, raw, kvs[1])
    terms = [moved(part, -1)]
    ds_list = [ds]
    for s in range(2, reach + 1):
        ds, part = next_past(s, share, start, q, g, stats, kvs[s])
        ds_list.append(ds)
        terms.append(moved(part, -s))
    query_grad, total = last_grads(share, start, q, g, stats, kvs, ds_list)
    key_grad, value_grad = sum_terms(total, terms)
    return (query_grad, key_grad, value_grad)


def solution(mesh):
    rows = P(("dp", "ctx"), "tp", None)
    stats = P("tp", "ctx", "dp")
    return jax.shard_map(
        local,
        mesh=mesh,
        in_specs=(rows, rows, rows, rows, stats, stats, P("dp")),
        out_specs=(rows, rows, rows),
        check_vma=False,
    )
```

```python
import functools

import jax
import jax.numpy as jnp
from jax import lax
from jax.experimental import pallas as pl
from jax.experimental.pallas import tpu as pltpu
from jax.sharding import PartitionSpec as P


DOC_MAX = 384
LOG2E = 1.4426950408889634
MIB = 1024 * 1024
VMEM = pl.BlockSpec(memory_space=pltpu.VMEM)
HBM = pl.BlockSpec(memory_space=pltpu.HBM)


def dot_nt(left, right):
    return lax.dot_general(left, right, (((1,), (1,)), ((), ())), preferred_element_type=jnp.float32)


def dot_nn(left, right):
    return lax.dot_general(left, right, (((1,), (0,)), ((), ())), preferred_element_type=jnp.float32)


def doc_start(docs_ref, token):
    start = jnp.zeros_like(token)
    end = jnp.int32(0)
    for d in range(docs_ref.shape[0]):
        end = end + docs_ref[d]
        start = jnp.where(token >= end, end, start)
    return start


def row_tokens(rows, share, first):
    return first + lax.broadcasted_iota(jnp.int32, (1, rows), 1) // share


def spread_stats(share, in_ref, out_ref):
    kv_heads, _, _, tok = in_ref.shape
    rows = tok * share
    x = in_ref[...].reshape(kv_heads * 2 * share, tok)
    high = x.astype(jnp.bfloat16)
    rest = x - high.astype(jnp.float32)
    mid = rest.astype(jnp.bfloat16)
    low = (rest - mid.astype(jnp.float32)).astype(jnp.bfloat16)
    at = lax.broadcasted_iota(jnp.int32, (tok, rows), 1) // share
    spread = (at == lax.broadcasted_iota(jnp.int32, (tok, rows), 0)).astype(jnp.float32)
    spread = spread.astype(jnp.bfloat16)
    parts = jnp.concatenate([high, mid, low], axis=1)
    y = dot_nn(parts, jnp.concatenate([spread] * 3, axis=0))
    own = lax.broadcasted_iota(jnp.int32, (share, rows), 1) % share
    own = own == lax.broadcasted_iota(jnp.int32, (share, rows), 0)
    for i in range(kv_heads):
        for j, factor in ((0, LOG2E), (1, 1.0)):
            first = (2 * i + j) * share
            row = jnp.sum(jnp.where(own, y[first : first + share], 0.0), axis=0, keepdims=True)
            out_ref[i, j : j + 1] = row * factor


def tile_grads(k, v, q, g, norm, delta, ok):
    scores = dot_nt(k, q)
    probs = jnp.exp2(scores * (q.shape[1] ** (-0.5) * LOG2E) - norm)
    if ok is not None:
        probs = jnp.where(ok, probs, 0.0)
    ds = (probs * (dot_nt(v, g) - delta)).astype(jnp.bfloat16)
    return ds, dot_nn(ds, q), dot_nn(probs.astype(jnp.bfloat16), g)


def head_rows(ref, i, share, first, count):
    block = ref[pl.ds(first, count), pl.ds(pl.multiple_of(i * share, share), share), :]
    return block.reshape(count * share, ref.shape[2])


def past_kernel(shift, share, start_ref, q_ref, g_ref, stats_ref, kv_ref, ds_ref, out_ref, acc_ref, ready):
    tok, _, dim = q_ref.shape
    _, kv_heads, keys, _ = kv_ref.shape
    scaling = dim ** (-0.5)
    base = (lax.axis_index("ctx") - shift) * keys
    none = (base < 0) | (jnp.min(start_ref[...]) >= base + keys)
    full = jnp.logical_not(none) & (jnp.max(start_ref[...]) <= base)

    @pl.when(full)
    def _():
        for i in range(kv_heads):
            ready(i)
            q = head_rows(q_ref, i, share, 0, tok)
            g = head_rows(g_ref, i, share, 0, tok)
            ds, dk, dv = tile_grads(
                kv_ref[0, i], kv_ref[1, i], q, g, stats_ref[i, 0:1], stats_ref[i, 1:2], None
            )
            ds_ref[i] = ds
            out_ref[0, i] = (dk * scaling).astype(out_ref.dtype)
            out_ref[1, i] = dv.astype(out_ref.dtype)

    @pl.when(jnp.logical_not(full))
    def _():
        for i in range(kv_heads):
            ready(i)

    @pl.when(none)
    def _():
        ds_ref[...] = jnp.zeros_like(ds_ref)
        out_ref[...] = jnp.zeros_like(out_ref)

    @pl.when(jnp.logical_not(none | full))
    def _():
        step = 32

        def one_head(i, _):
            acc_ref[...] = jnp.zeros_like(acc_ref)
            for b in range(tok // step):
                cut = slice(b * step * share, (b + 1) * step * share)
                start = start_ref[:, cut]
                reached = jnp.min(start) < base + keys

                @pl.when(reached)
                def _():
                    q = head_rows(q_ref, i, share, b * step, step)
                    g = head_rows(g_ref, i, share, b * step, step)
                    key = base + lax.broadcasted_iota(jnp.int32, (keys, step * share), 0)
                    ds, dk, dv = tile_grads(
                        kv_ref[0, i],
                        kv_ref[1, i],
                        q,
                        g,
                        stats_ref[i, 0:1, cut],
                        stats_ref[i, 1:2, cut],
                        key >= start,
                    )
                    ds_ref[i, :, cut] = ds
                    acc_ref[0] += dk
                    acc_ref[1] += dv

                @pl.when(jnp.logical_not(reached))
                def _():
                    ds_ref[i, :, cut] = jnp.zeros((keys, step * share), jnp.bfloat16)

            out_ref[0, i] = (acc_ref[0] * scaling).astype(out_ref.dtype)
            out_ref[1, i] = acc_ref[1].astype(out_ref.dtype)
            return 0

        lax.fori_loop(0, kv_heads, one_head, 0)


def first_past_kernel(share, docs_hbm, q_hbm, g_hbm, raw_ref, kv_ref, *refs):
    ds_ref, out_ref, q_ref, g_ref, stats_ref, start_ref, acc_ref, docs_ref, docs_sem, q_sem, g_sem = refs
    tok = q_ref.shape[0]

    def copies(i):
        heads = pl.ds(i * share, share)
        return (
            pltpu.make_async_copy(q_hbm.at[:, heads, :], q_ref.at[:, heads, :], q_sem.at[i]),
            pltpu.make_async_copy(g_hbm.at[:, heads, :], g_ref.at[:, heads, :], g_sem.at[i]),
        )

    def ready(i):
        for copy in copies(i):
            copy.wait()

    docs_copy = pltpu.make_async_copy(docs_hbm, docs_ref, docs_sem)
    docs_copy.start()
    for i in range(kv_ref.shape[1]):
        for copy in copies(i):
            copy.start()
    spread_stats(share, raw_ref, stats_ref)
    docs_copy.wait()
    token = row_tokens(tok * share, share, lax.axis_index("ctx") * tok)
    start_ref[...] = doc_start(docs_ref, token)
    past_kernel(1, share, start_ref, q_ref, g_ref, stats_ref, kv_ref, ds_ref, out_ref, acc_ref, ready)


def next_past_kernel(shift, share, *refs):
    past_kernel(shift, share, *refs, lambda i: None)


def past_cost(kv, rows):
    _, kv_heads, keys, dim = kv.shape
    return pl.CostEstimate(
        flops=8 * kv_heads * keys * rows * dim,
        transcendentals=kv_heads * keys * rows,
        bytes_accessed=4 * kv_heads * rows * dim,
    )


def in_hbm(*arrays):
    return [pltpu.with_memory_space_constraint(x, pltpu.HBM) for x in arrays]


def first_past(share, docs, q, g, raw, kv):
    _, kv_heads, keys, dim = kv.shape
    rows = q.shape[0] * share
    return pl.pallas_call(
        functools.partial(first_past_kernel, share),
        in_specs=[HBM, HBM, HBM, VMEM, VMEM],
        out_specs=[VMEM] * 6,
        out_shape=[
            jax.ShapeDtypeStruct((kv_heads, keys, rows), jnp.bfloat16),
            jax.ShapeDtypeStruct(kv.shape, jnp.float32),
            jax.ShapeDtypeStruct(q.shape, q.dtype),
            jax.ShapeDtypeStruct(g.shape, g.dtype),
            jax.ShapeDtypeStruct((kv_heads, 2, rows), jnp.float32),
            jax.ShapeDtypeStruct((1, rows), jnp.int32),
        ],
        scratch_shapes=[
            pltpu.VMEM((2, keys, dim), jnp.float32),
            pltpu.SMEM(docs.shape, jnp.int32),
            pltpu.SemaphoreType.DMA,
            pltpu.SemaphoreType.DMA((kv_heads,)),
            pltpu.SemaphoreType.DMA((kv_heads,)),
        ],
        compiler_params=pltpu.CompilerParams(vmem_limit_bytes=32 * MIB),
        cost_estimate=past_cost(kv, rows),
        name="past_1",
    )(*in_hbm(docs, q, g), raw, kv)


def next_past(shift, share, start, q, g, stats, kv):
    _, kv_heads, keys, dim = kv.shape
    rows = stats.shape[2]
    return pl.pallas_call(
        functools.partial(next_past_kernel, shift, share),
        in_specs=[VMEM] * 5,
        out_specs=[VMEM, VMEM],
        out_shape=[
            jax.ShapeDtypeStruct((kv_heads, keys, rows), jnp.bfloat16),
            jax.ShapeDtypeStruct(kv.shape, jnp.bfloat16),
        ],
        scratch_shapes=[pltpu.VMEM((2, keys, dim), jnp.float32)],
        compiler_params=pltpu.CompilerParams(vmem_limit_bytes=24 * MIB),
        cost_estimate=past_cost(kv, rows),
    )(start, q, g, stats, kv)


def last_kernel(share, start_ref, q_ref, g_ref, stats_ref, kv_ref, *refs):
    n = (len(refs) - 2) // 2
    past_kv, past_ds, (dq_ref, out_ref) = refs[:n], refs[n : 2 * n], refs[2 * n :]
    tok, _, dim = q_ref.shape
    _, kv_heads, keys, _ = kv_ref.shape
    rows = tok * share
    scaling = dim ** (-0.5)
    first = lax.axis_index("ctx") * tok
    key = first + lax.broadcasted_iota(jnp.int32, (keys, rows), 0)
    ok = (key >= start_ref[...]) & (key <= row_tokens(rows, share, first))
    for i in range(kv_heads):
        k = kv_ref[0, i]
        q = head_rows(q_ref, i, share, 0, tok)
        g = head_rows(g_ref, i, share, 0, tok)
        ds, dk, dv = tile_grads(k, kv_ref[1, i], q, g, stats_ref[i, 0:1], stats_ref[i, 1:2], ok)
        out_ref[0, i] = dk * scaling
        out_ref[1, i] = dv
        ks = jnp.concatenate([k] + [r[0, i] for r in past_kv], axis=0)
        ds = jnp.concatenate([ds] + [r[i] for r in past_ds], axis=0)
        dq = dot_nn(ks.T, ds) * scaling
        dq_ref[:, i * share : (i + 1) * share, :] = dq.T.astype(jnp.bfloat16).reshape(tok, share, dim)


def last_grads(share, start, q, g, stats, kvs, ds_list):
    _, kv_heads, keys, dim = kvs[0].shape
    rows = stats.shape[2]
    n = len(kvs)
    return pl.pallas_call(
        functools.partial(last_kernel, share),
        in_specs=[VMEM] * (4 + n + len(ds_list)),
        out_specs=[VMEM, VMEM],
        out_shape=[
            jax.ShapeDtypeStruct(q.shape, jnp.bfloat16),
            jax.ShapeDtypeStruct(kvs[0].shape, jnp.float32),
        ],
        compiler_params=pltpu.CompilerParams(vmem_limit_bytes=24 * MIB),
        cost_estimate=pl.CostEstimate(
            flops=(8 + 2 * n) * kv_heads * keys * rows * dim,
            transcendentals=kv_heads * keys * rows,
            bytes_accessed=4 * kv_heads * rows * dim,
        ),
        name="last",
    )(start, q, g, stats, *kvs, *ds_list)


def sum_kernel(*refs):
    own_ref, terms, (key_ref, value_ref) = refs[0], refs[1:-2], refs[-2:]
    for j, ref in enumerate((key_ref, value_ref)):
        total = own_ref[j]
        for term in terms:
            total = total + term[j].astype(jnp.float32)
        ref[...] = jnp.swapaxes(total, 0, 1).astype(jnp.bfloat16)


def sum_terms(own, terms):
    _, kv_heads, keys, dim = own.shape
    return pl.pallas_call(
        sum_kernel,
        in_specs=[VMEM] * (1 + len(terms)),
        out_shape=[jax.ShapeDtypeStruct((keys, kv_heads, dim), jnp.bfloat16)] * 2,
        compiler_params=pltpu.CompilerParams(vmem_limit_bytes=24 * MIB),
        name="sum",
    )(own, *terms)


def local(query_rows, key_rows, value_rows, out_grad, softmax_delta, log_norm, doc_lengths):
    groups = lax.axis_size("ctx")
    tok, heads, _ = query_rows.shape
    kv_heads = key_rows.shape[1]
    share = heads // kv_heads
    per_dev = heads // groups
    reach = min(groups - 1, -(-(DOC_MAX - 1) // tok))

    def moved(x, s, first=0):
        pairs = [(i, i + s) for i in range(first, groups) if 0 <= i + s < groups]
        return lax.ppermute(x, "ctx", pairs)

    kvs = [jnp.stack([key_rows, value_rows]).transpose(0, 2, 1, 3)]
    for s in range(1, reach + 1):
        kvs.append(moved(kvs[1], 1, 1) if s == 2 else moved(kvs[0], s))
    raw = jnp.stack([log_norm[0], softmax_delta[0]])
    raw = raw.reshape(2, per_dev, groups, tok).transpose(2, 0, 1, 3)
    raw = lax.all_to_all(raw, "ctx", split_axis=0, concat_axis=0, tiled=True)
    raw = raw.reshape(kv_heads, groups // kv_heads, 2, per_dev, tok)
    raw = raw.transpose(0, 2, 1, 3, 4).reshape(kv_heads, 2, share, tok)
    ds, near, q, g, stats, start = first_past(share, doc_lengths, query_rows, out_grad, raw, kvs[1])
    ds_list, terms = [ds], []
    for s in range(2, reach + 1):
        ds, part = next_past(s, share, start, q, g, stats, kvs[s])
        ds_list.append(ds)
        if s == 2:
            near = near + moved(part, -1, 2).astype(jnp.float32)
        else:
            terms.append(moved(part, -s))
    terms.append(moved(near.astype(jnp.bfloat16), -1))
    query_grad, total = last_grads(share, start, q, g, stats, kvs, ds_list)
    key_grad, value_grad = sum_terms(total, terms)
    return (query_grad, key_grad, value_grad)


def solution(mesh):
    rows = P(("dp", "ctx"), "tp", None)
    stats = P("tp", "ctx", "dp")
    return jax.shard_map(
        local,
        mesh=mesh,
        in_specs=(rows, rows, rows, rows, stats, stats, P("dp")),
        out_specs=(rows, rows, rows),
        check_vma=False,
    )
```

```python
import functools

import jax
import jax.numpy as jnp
from jax import lax
from jax.experimental import pallas as pl
from jax.experimental.pallas import tpu as pltpu
from jax.sharding import PartitionSpec as P


DOC_MAX = 384
LOG2E = 1.4426950408889634
MIB = 1024 * 1024
VMEM = pl.BlockSpec(memory_space=pltpu.VMEM)
HBM = pl.BlockSpec(memory_space=pltpu.HBM)


def dot_nt(left, right):
    return lax.dot_general(left, right, (((1,), (1,)), ((), ())), preferred_element_type=jnp.float32)


def dot_nn(left, right):
    return lax.dot_general(left, right, (((1,), (0,)), ((), ())), preferred_element_type=jnp.float32)


def doc_start(docs_ref, token):
    start = jnp.zeros_like(token)
    end = jnp.int32(0)
    for d in range(docs_ref.shape[0]):
        end = end + docs_ref[d]
        start = jnp.where(token >= end, end, start)
    return start


def row_tokens(rows, share, first):
    return first + lax.broadcasted_iota(jnp.int32, (1, rows), 1) // share


def spread_stats(share, in_ref, out_ref):
    kv_heads, _, _, tok = in_ref.shape
    rows = tok * share
    x = in_ref[...].reshape(kv_heads * 2 * share, tok)
    high = x.astype(jnp.bfloat16)
    rest = x - high.astype(jnp.float32)
    mid = rest.astype(jnp.bfloat16)
    low = (rest - mid.astype(jnp.float32)).astype(jnp.bfloat16)
    at = lax.broadcasted_iota(jnp.int32, (tok, rows), 1) // share
    spread = (at == lax.broadcasted_iota(jnp.int32, (tok, rows), 0)).astype(jnp.float32)
    spread = spread.astype(jnp.bfloat16)
    parts = jnp.concatenate([high, mid, low], axis=1)
    y = dot_nn(parts, jnp.concatenate([spread] * 3, axis=0))
    own = lax.broadcasted_iota(jnp.int32, (share, rows), 1) % share
    own = own == lax.broadcasted_iota(jnp.int32, (share, rows), 0)
    for i in range(kv_heads):
        for j, factor in ((0, LOG2E), (1, 1.0)):
            first = (2 * i + j) * share
            row = jnp.sum(jnp.where(own, y[first : first + share], 0.0), axis=0, keepdims=True)
            out_ref[i, j : j + 1] = row * factor


def tile_grads(k, v, q, g, norm, delta, ok):
    scores = dot_nt(k, q)
    probs = jnp.exp2(scores * (q.shape[1] ** (-0.5) * LOG2E) - norm)
    if ok is not None:
        probs = jnp.where(ok, probs, 0.0)
    ds = (probs * (dot_nt(v, g) - delta)).astype(jnp.bfloat16)
    return ds, dot_nn(ds, q), dot_nn(probs.astype(jnp.bfloat16), g)


def head_rows(ref, i, share, first, count):
    block = ref[pl.ds(first, count), pl.ds(pl.multiple_of(i * share, share), share), :]
    return block.reshape(count * share, ref.shape[2])


def past_kernel(shift, share, lead, start_ref, q_ref, g_ref, stats_ref, kv_ref, ds_ref, outs, acc_ref, ready):
    tok, _, dim = q_ref.shape
    kv_heads, keys, _ = ds_ref.shape
    scaling = dim ** (-0.5)
    base = (lax.axis_index("ctx") - shift) * keys
    none = (base < 0) | (jnp.min(start_ref[...]) >= base + keys)
    full = jnp.logical_not(none) & (jnp.max(start_ref[...]) <= base)

    @pl.when(full)
    def _():
        for i in range(kv_heads):
            ready(i)
            q = head_rows(q_ref, lead + i, share, 0, tok)
            g = head_rows(g_ref, lead + i, share, 0, tok)
            ds, dk, dv = tile_grads(
                kv_ref[0, lead + i], kv_ref[1, lead + i], q, g, stats_ref[lead + i, 0:1], stats_ref[lead + i, 1:2], None
            )
            ds_ref[i] = ds
            out_ref = outs[i // outs[0].shape[1]]
            at = i % outs[0].shape[1]
            out_ref[0, at] = (dk * scaling).astype(out_ref.dtype)
            out_ref[1, at] = dv.astype(out_ref.dtype)

    @pl.when(jnp.logical_not(full))
    def _():
        for i in range(kv_heads):
            ready(i)

    @pl.when(none)
    def _():
        ds_ref[...] = jnp.zeros_like(ds_ref)
        for out_ref in outs:
            out_ref[...] = jnp.zeros_like(out_ref)

    @pl.when(jnp.logical_not(none | full))
    def _():
        step = 32

        def masked_head(out_ref, skip, i, _):
            acc_ref[...] = jnp.zeros_like(acc_ref)
            for b in range(tok // step):
                cut = slice(b * step * share, (b + 1) * step * share)
                start = start_ref[:, cut]
                reached = jnp.min(start) < base + keys

                @pl.when(reached)
                def _():
                    q = head_rows(q_ref, lead + i, share, b * step, step)
                    g = head_rows(g_ref, lead + i, share, b * step, step)
                    key = base + lax.broadcasted_iota(jnp.int32, (keys, step * share), 0)
                    ds, dk, dv = tile_grads(
                        kv_ref[0, lead + i],
                        kv_ref[1, lead + i],
                        q,
                        g,
                        stats_ref[lead + i, 0:1, cut],
                        stats_ref[lead + i, 1:2, cut],
                        key >= start,
                    )
                    ds_ref[i, :, cut] = ds
                    acc_ref[0] += dk
                    acc_ref[1] += dv

                @pl.when(jnp.logical_not(reached))
                def _():
                    ds_ref[i, :, cut] = jnp.zeros((keys, step * share), jnp.bfloat16)

            out_ref[0, i - skip] = (acc_ref[0] * scaling).astype(out_ref.dtype)
            out_ref[1, i - skip] = acc_ref[1].astype(out_ref.dtype)
            return 0

        for j, out_ref in enumerate(outs):
            skip = j * out_ref.shape[1]
            one_head = functools.partial(masked_head, out_ref, skip)
            lax.fori_loop(skip, skip + out_ref.shape[1], one_head, 0)


def first_past_kernel(share, docs_hbm, q_hbm, g_hbm, raw_ref, kv_ref, *refs):
    ds_ref, *outs = refs[:-9]
    q_ref, g_ref, stats_ref, start_ref, acc_ref, docs_ref, docs_sem, q_sem, g_sem = refs[-9:]
    tok = q_ref.shape[0]

    def copies(i):
        heads = pl.ds(i * share, share)
        return (
            pltpu.make_async_copy(q_hbm.at[:, heads, :], q_ref.at[:, heads, :], q_sem.at[i]),
            pltpu.make_async_copy(g_hbm.at[:, heads, :], g_ref.at[:, heads, :], g_sem.at[i]),
        )

    def ready(i):
        for copy in copies(i):
            copy.wait()

    docs_copy = pltpu.make_async_copy(docs_hbm, docs_ref, docs_sem)
    docs_copy.start()
    for i in range(kv_ref.shape[1]):
        for copy in copies(i):
            copy.start()
    spread_stats(share, raw_ref, stats_ref)
    docs_copy.wait()
    token = row_tokens(tok * share, share, lax.axis_index("ctx") * tok)
    start_ref[...] = doc_start(docs_ref, token)
    past_kernel(1, share, 0, start_ref, q_ref, g_ref, stats_ref, kv_ref, ds_ref, outs, acc_ref, ready)


def next_past_kernel(shift, share, lead, *refs):
    *ins, out_ref, acc_ref = refs
    past_kernel(shift, share, lead, *ins, [out_ref], acc_ref, lambda i: None)


def past_cost(kv_heads, keys, rows, dim):
    return pl.CostEstimate(
        flops=8 * kv_heads * keys * rows * dim,
        transcendentals=kv_heads * keys * rows,
        bytes_accessed=4 * kv_heads * rows * dim,
    )


def in_hbm(*arrays):
    return [pltpu.with_memory_space_constraint(x, pltpu.HBM) for x in arrays]


def first_past(share, halves, docs, q, g, raw, kv):
    _, kv_heads, keys, dim = kv.shape
    rows = q.shape[0] * share
    return pl.pallas_call(
        functools.partial(first_past_kernel, share),
        in_specs=[HBM, HBM, HBM, VMEM, VMEM],
        out_specs=[VMEM] * (5 + halves),
        out_shape=[
            jax.ShapeDtypeStruct((kv_heads, keys, rows), jnp.bfloat16),
        ]
        + [jax.ShapeDtypeStruct((2, kv_heads // halves, keys, dim), jnp.float32)] * halves
        + [
            jax.ShapeDtypeStruct(q.shape, q.dtype),
            jax.ShapeDtypeStruct(g.shape, g.dtype),
            jax.ShapeDtypeStruct((kv_heads, 2, rows), jnp.float32),
            jax.ShapeDtypeStruct((1, rows), jnp.int32),
        ],
        scratch_shapes=[
            pltpu.VMEM((2, keys, dim), jnp.float32),
            pltpu.SMEM(docs.shape, jnp.int32),
            pltpu.SemaphoreType.DMA,
            pltpu.SemaphoreType.DMA((kv_heads,)),
            pltpu.SemaphoreType.DMA((kv_heads,)),
        ],
        compiler_params=pltpu.CompilerParams(vmem_limit_bytes=32 * MIB),
        cost_estimate=past_cost(kv_heads, keys, rows, dim),
        name="past_1",
    )(*in_hbm(docs, q, g), raw, kv)


def next_past(shift, share, lead, kv_heads, start, q, g, stats, kv):
    _, _, keys, dim = kv.shape
    rows = stats.shape[2]
    return pl.pallas_call(
        functools.partial(next_past_kernel, shift, share, lead),
        in_specs=[VMEM] * 5,
        out_specs=[VMEM, VMEM],
        out_shape=[
            jax.ShapeDtypeStruct((kv_heads, keys, rows), jnp.bfloat16),
            jax.ShapeDtypeStruct((2, kv_heads, keys, dim), jnp.bfloat16),
        ],
        scratch_shapes=[pltpu.VMEM((2, keys, dim), jnp.float32)],
        compiler_params=pltpu.CompilerParams(vmem_limit_bytes=24 * MIB),
        cost_estimate=past_cost(kv_heads, keys, rows, dim),
    )(start, q, g, stats, kv)


def grouped(items, counts):
    groups, at = [], 0
    for count in counts:
        groups.append(items[at : at + count])
        at += count
    return groups


def own_kernel(share, start_ref, q_ref, g_ref, stats_ref, kv_ref, ds_ref, out_ref):
    tok, _, dim = q_ref.shape
    _, kv_heads, keys, _ = kv_ref.shape
    rows = tok * share
    scaling = dim ** (-0.5)
    first = lax.axis_index("ctx") * tok
    key = first + lax.broadcasted_iota(jnp.int32, (keys, rows), 0)
    ok = (key >= start_ref[...]) & (key <= row_tokens(rows, share, first))
    for i in range(kv_heads):
        q = head_rows(q_ref, i, share, 0, tok)
        g = head_rows(g_ref, i, share, 0, tok)
        ds, dk, dv = tile_grads(
            kv_ref[0, i], kv_ref[1, i], q, g, stats_ref[i, 0:1], stats_ref[i, 1:2], ok
        )
        ds_ref[i] = ds
        out_ref[0, i] = dk * scaling
        out_ref[1, i] = dv


def own_grads(share, start, q, g, stats, kv):
    _, kv_heads, keys, dim = kv.shape
    rows = stats.shape[2]
    return pl.pallas_call(
        functools.partial(own_kernel, share),
        in_specs=[VMEM] * 5,
        out_specs=[VMEM, VMEM],
        out_shape=[
            jax.ShapeDtypeStruct((kv_heads, keys, rows), jnp.bfloat16),
            jax.ShapeDtypeStruct(kv.shape, jnp.float32),
        ],
        compiler_params=pltpu.CompilerParams(vmem_limit_bytes=24 * MIB),
        cost_estimate=past_cost(kv_heads, keys, rows, dim),
        name="own",
    )(start, q, g, stats, kv)


def query_kernel(share, counts, *refs):
    n = len(counts)
    kvs, ds_refs, dq_ref = refs[:n], grouped(refs[n:-1], counts), refs[-1]
    tok, _, dim = dq_ref.shape
    scaling = dim ** (-0.5)
    for i in range(kvs[0].shape[1]):
        pieces = [r[i // r[0].shape[0]] for r in ds_refs]
        ks = jnp.concatenate([r[0, i] for r in kvs], axis=0)
        ds = jnp.concatenate([r[i % r.shape[0]] for r in pieces], axis=0)
        dq = dot_nn(ks.T, ds) * scaling
        dq_ref[:, i * share : (i + 1) * share, :] = dq.T.astype(jnp.bfloat16).reshape(tok, share, dim)


def query_grads(share, tok, kvs, ds_list):
    _, kv_heads, keys, dim = kvs[0].shape
    rows = tok * share
    n = len(kvs)
    counts = tuple(len(pieces) for pieces in ds_list)
    return pl.pallas_call(
        functools.partial(query_kernel, share, counts),
        in_specs=[VMEM] * (n + sum(counts)),
        out_specs=VMEM,
        out_shape=jax.ShapeDtypeStruct((tok, kv_heads * share, dim), jnp.bfloat16),
        compiler_params=pltpu.CompilerParams(vmem_limit_bytes=24 * MIB),
        cost_estimate=pl.CostEstimate(
            flops=2 * n * kv_heads * keys * rows * dim,
            transcendentals=0,
            bytes_accessed=2 * n * kv_heads * rows * dim,
        ),
        name="query",
    )(*kvs, *sum(ds_list, ()))


def sum_kernel(counts, *refs):
    own_ref, terms, (key_ref, value_ref) = refs[0], grouped(refs[1:-2], counts), refs[-2:]
    for j, ref in enumerate((key_ref, value_ref)):
        total = own_ref[j]
        for pieces in terms:
            term = jnp.concatenate([piece[j] for piece in pieces], axis=0)
            total = total + term.astype(jnp.float32)
        ref[...] = jnp.swapaxes(total.astype(jnp.bfloat16), 0, 1)


def sum_terms(own, terms):
    _, kv_heads, keys, dim = own.shape
    counts = tuple(len(pieces) for pieces in terms)
    return pl.pallas_call(
        functools.partial(sum_kernel, counts),
        in_specs=[VMEM] * (1 + sum(counts)),
        out_shape=[jax.ShapeDtypeStruct((keys, kv_heads, dim), jnp.bfloat16)] * 2,
        compiler_params=pltpu.CompilerParams(vmem_limit_bytes=24 * MIB),
        name="sum",
    )(own, *sum(terms, ()))


def local(query_rows, key_rows, value_rows, out_grad, softmax_delta, log_norm, doc_lengths):
    groups = lax.axis_size("ctx")
    tok, heads, _ = query_rows.shape
    kv_heads = key_rows.shape[1]
    share = heads // kv_heads
    per_dev = heads // groups
    reach = min(groups - 1, -(-(DOC_MAX - 1) // tok))

    def moved(x, s, first=0):
        pairs = [(i, i + s) for i in range(first, groups) if 0 <= i + s < groups]
        return lax.ppermute(x, "ctx", pairs)

    kvs = [jnp.stack([key_rows, value_rows]).transpose(0, 2, 1, 3)]
    for s in range(1, reach + 1):
        kvs.append(moved(kvs[1], 1, 1) if s == 2 else moved(kvs[0], s))
    raw = jnp.stack([log_norm[0], softmax_delta[0]])
    raw = raw.reshape(2, per_dev, groups, tok).transpose(2, 0, 1, 3)
    raw = lax.all_to_all(raw, "ctx", split_axis=0, concat_axis=0, tiled=True)
    raw = raw.reshape(kv_heads, groups // kv_heads, 2, per_dev, tok)
    raw = raw.transpose(0, 2, 1, 3, 4).reshape(kv_heads, 2, share, tok)
    halves = 2 if kv_heads % 2 == 0 else 1
    ds, *near, q, g, stats, start = first_past(
        share, halves, doc_lengths, query_rows, out_grad, raw, kvs[1]
    )
    part = kv_heads // halves
    ds_list, terms, hops = [(ds,)], [], []
    if reach >= 2:
        pieces = []
        for h in range(halves):
            ds, term = next_past(2, share, h * part, part, start, q, g, stats, kvs[2])
            pieces.append(ds)
            hops.append(moved(term, -1, 2))
        ds_list.append(tuple(pieces))
    for s in range(3, reach + 1):
        ds, term = next_past(s, share, 0, kv_heads, start, q, g, stats, kvs[s])
        ds_list.append((ds,))
        terms.append((moved(term, -s),))
    pieces = []
    for h in range(halves):
        term = near[h]
        if hops:
            term = term + hops[h].astype(jnp.float32)
        pieces.append(moved(term.astype(jnp.bfloat16), -1))
    terms.append(tuple(pieces))
    ds, total = own_grads(share, start, q, g, stats, kvs[0])
    ds_list.insert(0, (ds,))
    query_grad = query_grads(share, tok, kvs, ds_list)
    key_grad, value_grad = sum_terms(total, terms)
    return (query_grad, key_grad, value_grad)


def solution(mesh):
    rows = P(("dp", "ctx"), "tp", None)
    stats = P("tp", "ctx", "dp")
    return jax.shard_map(
        local,
        mesh=mesh,
        in_specs=(rows, rows, rows, rows, stats, stats, P("dp")),
        out_specs=(rows, rows, rows),
        check_vma=False,
    )
```

```python
import functools

import jax
import jax.numpy as jnp
from jax import lax
from jax.experimental import pallas as pl
from jax.experimental.pallas import tpu as pltpu
from jax.sharding import PartitionSpec as P


DOC_MAX = 384
LOG2E = 1.4426950408889634
MIB = 1024 * 1024
VMEM = pl.BlockSpec(memory_space=pltpu.VMEM)
HBM = pl.BlockSpec(memory_space=pltpu.HBM)


def dot_nt(left, right):
    return lax.dot_general(left, right, (((1,), (1,)), ((), ())), preferred_element_type=jnp.float32)


def dot_nn(left, right):
    return lax.dot_general(left, right, (((1,), (0,)), ((), ())), preferred_element_type=jnp.float32)


def doc_start(docs_ref, token):
    start = jnp.zeros_like(token)
    end = jnp.int32(0)
    for d in range(docs_ref.shape[0]):
        end = end + docs_ref[d]
        start = jnp.where(token >= end, end, start)
    return start


def row_tokens(rows, share, first):
    return first + lax.broadcasted_iota(jnp.int32, (1, rows), 1) // share


def spread_stats(share, in_ref, out_ref):
    kv_heads, _, _, tok = in_ref.shape
    rows = tok * share
    x = in_ref[...].reshape(kv_heads * 2 * share, tok)
    high = x.astype(jnp.bfloat16)
    rest = x - high.astype(jnp.float32)
    mid = rest.astype(jnp.bfloat16)
    low = (rest - mid.astype(jnp.float32)).astype(jnp.bfloat16)
    at = lax.broadcasted_iota(jnp.int32, (tok, rows), 1) // share
    spread = (at == lax.broadcasted_iota(jnp.int32, (tok, rows), 0)).astype(jnp.float32)
    spread = spread.astype(jnp.bfloat16)
    parts = jnp.concatenate([high, mid, low], axis=1)
    y = dot_nn(parts, jnp.concatenate([spread] * 3, axis=0))
    own = lax.broadcasted_iota(jnp.int32, (share, rows), 1) % share
    own = own == lax.broadcasted_iota(jnp.int32, (share, rows), 0)
    for i in range(kv_heads):
        for j, factor in ((0, LOG2E), (1, 1.0)):
            first = (2 * i + j) * share
            row = jnp.sum(jnp.where(own, y[first : first + share], 0.0), axis=0, keepdims=True)
            out_ref[i, j : j + 1] = row * factor


def tile_grads(k, v, q, g, norm, delta, ok):
    scores = dot_nt(k, q)
    probs = jnp.exp2(scores * (q.shape[1] ** (-0.5) * LOG2E) - norm)
    if ok is not None:
        probs = jnp.where(ok, probs, 0.0)
    ds = (probs * (dot_nt(v, g) - delta)).astype(jnp.bfloat16)
    return ds, dot_nn(ds, q), dot_nn(probs.astype(jnp.bfloat16), g)


def head_rows(ref, i, share, first, count):
    block = ref[pl.ds(first, count), pl.ds(pl.multiple_of(i * share, share), share), :]
    return block.reshape(count * share, ref.shape[2])


def past_kernel(shift, share, lead, start_ref, q_ref, g_ref, stats_ref, kv_ref, ds_ref, outs, acc_ref, ready):
    tok, _, dim = q_ref.shape
    kv_heads, keys, _ = ds_ref.shape
    scaling = dim ** (-0.5)
    base = (lax.axis_index("ctx") - shift) * keys
    none = (base < 0) | (jnp.min(start_ref[...]) >= base + keys)
    full = jnp.logical_not(none) & (jnp.max(start_ref[...]) <= base)

    @pl.when(full)
    def _():
        for i in range(kv_heads):
            ready(i)
            q = head_rows(q_ref, lead + i, share, 0, tok)
            g = head_rows(g_ref, lead + i, share, 0, tok)
            ds, dk, dv = tile_grads(
                kv_ref[0, lead + i], kv_ref[1, lead + i], q, g, stats_ref[lead + i, 0:1], stats_ref[lead + i, 1:2], None
            )
            ds_ref[i] = ds
            out_ref = outs[i // outs[0].shape[1]]
            at = i % outs[0].shape[1]
            out_ref[0, at] = (dk * scaling).astype(out_ref.dtype)
            out_ref[1, at] = dv.astype(out_ref.dtype)

    @pl.when(jnp.logical_not(full))
    def _():
        for i in range(kv_heads):
            ready(i)

    @pl.when(none)
    def _():
        ds_ref[...] = jnp.zeros_like(ds_ref)
        for out_ref in outs:
            out_ref[...] = jnp.zeros_like(out_ref)

    @pl.when(jnp.logical_not(none | full))
    def _():
        step = 32

        def masked_head(out_ref, skip, i, _):
            acc_ref[...] = jnp.zeros_like(acc_ref)
            for b in range(tok // step):
                cut = slice(b * step * share, (b + 1) * step * share)
                start = start_ref[:, cut]
                reached = jnp.min(start) < base + keys

                @pl.when(reached)
                def _():
                    q = head_rows(q_ref, lead + i, share, b * step, step)
                    g = head_rows(g_ref, lead + i, share, b * step, step)
                    key = base + lax.broadcasted_iota(jnp.int32, (keys, step * share), 0)
                    ds, dk, dv = tile_grads(
                        kv_ref[0, lead + i],
                        kv_ref[1, lead + i],
                        q,
                        g,
                        stats_ref[lead + i, 0:1, cut],
                        stats_ref[lead + i, 1:2, cut],
                        key >= start,
                    )
                    ds_ref[i, :, cut] = ds
                    acc_ref[0] += dk
                    acc_ref[1] += dv

                @pl.when(jnp.logical_not(reached))
                def _():
                    ds_ref[i, :, cut] = jnp.zeros((keys, step * share), jnp.bfloat16)

            out_ref[0, i - skip] = (acc_ref[0] * scaling).astype(out_ref.dtype)
            out_ref[1, i - skip] = acc_ref[1].astype(out_ref.dtype)
            return 0

        for j, out_ref in enumerate(outs):
            skip = j * out_ref.shape[1]
            one_head = functools.partial(masked_head, out_ref, skip)
            lax.fori_loop(skip, skip + out_ref.shape[1], one_head, 0)


def first_past_kernel(share, docs_hbm, q_hbm, g_hbm, raw_ref, kv_ref, *refs):
    ds_ref, *outs = refs[:-9]
    q_ref, g_ref, stats_ref, start_ref, acc_ref, docs_ref, docs_sem, q_sem, g_sem = refs[-9:]
    tok = q_ref.shape[0]

    def copies(i):
        heads = pl.ds(i * share, share)
        return (
            pltpu.make_async_copy(q_hbm.at[:, heads, :], q_ref.at[:, heads, :], q_sem.at[i]),
            pltpu.make_async_copy(g_hbm.at[:, heads, :], g_ref.at[:, heads, :], g_sem.at[i]),
        )

    def ready(i):
        for copy in copies(i):
            copy.wait()

    docs_copy = pltpu.make_async_copy(docs_hbm, docs_ref, docs_sem)
    docs_copy.start()
    for i in range(kv_ref.shape[1]):
        for copy in copies(i):
            copy.start()
    spread_stats(share, raw_ref, stats_ref)
    docs_copy.wait()
    token = row_tokens(tok * share, share, lax.axis_index("ctx") * tok)
    start_ref[...] = doc_start(docs_ref, token)
    past_kernel(1, share, 0, start_ref, q_ref, g_ref, stats_ref, kv_ref, ds_ref, outs, acc_ref, ready)


def next_past_kernel(shift, share, lead, *refs):
    *ins, out_ref, acc_ref = refs
    past_kernel(shift, share, lead, *ins, [out_ref], acc_ref, lambda i: None)


def past_cost(kv_heads, keys, rows, dim):
    return pl.CostEstimate(
        flops=8 * kv_heads * keys * rows * dim,
        transcendentals=kv_heads * keys * rows,
        bytes_accessed=4 * kv_heads * rows * dim,
    )


def in_hbm(*arrays):
    return [pltpu.with_memory_space_constraint(x, pltpu.HBM) for x in arrays]


def first_past(share, halves, docs, q, g, raw, kv):
    _, kv_heads, keys, dim = kv.shape
    rows = q.shape[0] * share
    return pl.pallas_call(
        functools.partial(first_past_kernel, share),
        in_specs=[HBM, HBM, HBM, VMEM, VMEM],
        out_specs=[VMEM] * (5 + halves),
        out_shape=[
            jax.ShapeDtypeStruct((kv_heads, keys, rows), jnp.bfloat16),
        ]
        + [jax.ShapeDtypeStruct((2, kv_heads // halves, keys, dim), jnp.float32)] * halves
        + [
            jax.ShapeDtypeStruct(q.shape, q.dtype),
            jax.ShapeDtypeStruct(g.shape, g.dtype),
            jax.ShapeDtypeStruct((kv_heads, 2, rows), jnp.float32),
            jax.ShapeDtypeStruct((1, rows), jnp.int32),
        ],
        scratch_shapes=[
            pltpu.VMEM((2, keys, dim), jnp.float32),
            pltpu.SMEM(docs.shape, jnp.int32),
            pltpu.SemaphoreType.DMA,
            pltpu.SemaphoreType.DMA((kv_heads,)),
            pltpu.SemaphoreType.DMA((kv_heads,)),
        ],
        compiler_params=pltpu.CompilerParams(vmem_limit_bytes=32 * MIB),
        cost_estimate=past_cost(kv_heads, keys, rows, dim),
        name="past_1",
    )(*in_hbm(docs, q, g), raw, kv)


def next_past(shift, share, lead, kv_heads, start, q, g, stats, kv):
    _, _, keys, dim = kv.shape
    rows = stats.shape[2]
    return pl.pallas_call(
        functools.partial(next_past_kernel, shift, share, lead),
        in_specs=[VMEM] * 5,
        out_specs=[VMEM, VMEM],
        out_shape=[
            jax.ShapeDtypeStruct((kv_heads, keys, rows), jnp.bfloat16),
            jax.ShapeDtypeStruct((2, kv_heads, keys, dim), jnp.bfloat16),
        ],
        scratch_shapes=[pltpu.VMEM((2, keys, dim), jnp.float32)],
        compiler_params=pltpu.CompilerParams(vmem_limit_bytes=24 * MIB),
        cost_estimate=past_cost(kv_heads, keys, rows, dim),
    )(start, q, g, stats, kv)


def grouped(items, counts):
    groups, at = [], 0
    for count in counts:
        groups.append(items[at : at + count])
        at += count
    return groups


def last_kernel(share, counts, start_ref, q_ref, g_ref, stats_ref, kv_ref, *refs):
    n = len(counts)
    past_kv, past_ds, (dq_ref, out_ref) = refs[:n], grouped(refs[n:-2], counts), refs[-2:]
    tok, _, dim = q_ref.shape
    _, kv_heads, keys, _ = kv_ref.shape
    rows = tok * share
    scaling = dim ** (-0.5)
    first = lax.axis_index("ctx") * tok
    key = first + lax.broadcasted_iota(jnp.int32, (keys, rows), 0)
    ok = (key >= start_ref[...]) & (key <= row_tokens(rows, share, first))
    for i in range(kv_heads):
        k = kv_ref[0, i]
        q = head_rows(q_ref, i, share, 0, tok)
        g = head_rows(g_ref, i, share, 0, tok)
        ds, dk, dv = tile_grads(k, kv_ref[1, i], q, g, stats_ref[i, 0:1], stats_ref[i, 1:2], ok)
        out_ref[0, i] = dk * scaling
        out_ref[1, i] = dv
        ks = jnp.concatenate([k] + [r[0, i] for r in past_kv], axis=0)
        pieces = [r[i // r[0].shape[0]] for r in past_ds]
        ds = jnp.concatenate([ds] + [r[i % r.shape[0]] for r in pieces], axis=0)
        dq = dot_nn(ks.T, ds) * scaling
        dq_ref[:, i * share : (i + 1) * share, :] = dq.T.astype(jnp.bfloat16).reshape(tok, share, dim)


def last_grads(share, start, q, g, stats, kvs, ds_list):
    _, kv_heads, keys, dim = kvs[0].shape
    rows = stats.shape[2]
    n = len(kvs)
    counts = tuple(len(pieces) for pieces in ds_list)
    return pl.pallas_call(
        functools.partial(last_kernel, share, counts),
        in_specs=[VMEM] * (4 + n + sum(counts)),
        out_specs=[VMEM, VMEM],
        out_shape=[
            jax.ShapeDtypeStruct(q.shape, jnp.bfloat16),
            jax.ShapeDtypeStruct(kvs[0].shape, jnp.float32),
        ],
        compiler_params=pltpu.CompilerParams(vmem_limit_bytes=24 * MIB),
        cost_estimate=pl.CostEstimate(
            flops=(8 + 2 * n) * kv_heads * keys * rows * dim,
            transcendentals=kv_heads * keys * rows,
            bytes_accessed=4 * kv_heads * rows * dim,
        ),
        name="last",
    )(start, q, g, stats, *kvs, *sum(ds_list, ()))


def sum_kernel(counts, *refs):
    own_ref, terms, (key_ref, value_ref) = refs[0], grouped(refs[1:-2], counts), refs[-2:]
    for j, ref in enumerate((key_ref, value_ref)):
        total = own_ref[j]
        for pieces in terms:
            term = jnp.concatenate([piece[j] for piece in pieces], axis=0)
            total = total + term.astype(jnp.float32)
        ref[...] = jnp.swapaxes(total.astype(jnp.bfloat16), 0, 1)


def sum_terms(own, terms):
    _, kv_heads, keys, dim = own.shape
    counts = tuple(len(pieces) for pieces in terms)
    return pl.pallas_call(
        functools.partial(sum_kernel, counts),
        in_specs=[VMEM] * (1 + sum(counts)),
        out_shape=[jax.ShapeDtypeStruct((keys, kv_heads, dim), jnp.bfloat16)] * 2,
        compiler_params=pltpu.CompilerParams(vmem_limit_bytes=24 * MIB),
        name="sum",
    )(own, *sum(terms, ()))


def local(query_rows, key_rows, value_rows, out_grad, softmax_delta, log_norm, doc_lengths):
    groups = lax.axis_size("ctx")
    tok, heads, _ = query_rows.shape
    kv_heads = key_rows.shape[1]
    share = heads // kv_heads
    per_dev = heads // groups
    reach = min(groups - 1, -(-(DOC_MAX - 1) // tok))

    def moved(x, s, first=0):
        pairs = [(i, i + s) for i in range(first, groups) if 0 <= i + s < groups]
        return lax.ppermute(x, "ctx", pairs)

    kvs = [jnp.stack([key_rows, value_rows]).transpose(0, 2, 1, 3)]
    for s in range(1, reach + 1):
        kvs.append(moved(kvs[1], 1, 1) if s == 2 else moved(kvs[0], s))
    raw = jnp.stack([log_norm[0], softmax_delta[0]])
    raw = raw.reshape(2, per_dev, groups, tok).transpose(2, 0, 1, 3)
    raw = lax.all_to_all(raw, "ctx", split_axis=0, concat_axis=0, tiled=True)
    raw = raw.reshape(kv_heads, groups // kv_heads, 2, per_dev, tok)
    raw = raw.transpose(0, 2, 1, 3, 4).reshape(kv_heads, 2, share, tok)
    halves = 2 if kv_heads % 2 == 0 else 1
    ds, *near, q, g, stats, start = first_past(
        share, halves, doc_lengths, query_rows, out_grad, raw, kvs[1]
    )
    part = kv_heads // halves
    ds_list, terms, hops = [(ds,)], [], []
    if reach >= 2:
        pieces = []
        for h in range(halves):
            ds, term = next_past(2, share, h * part, part, start, q, g, stats, kvs[2])
            pieces.append(ds)
            hops.append(moved(term, -1, 2))
        ds_list.append(tuple(pieces))
    for s in range(3, reach + 1):
        ds, term = next_past(s, share, 0, kv_heads, start, q, g, stats, kvs[s])
        ds_list.append((ds,))
        terms.append((moved(term, -s),))
    pieces = []
    for h in range(halves):
        term = near[h]
        if hops:
            term = term + hops[h].astype(jnp.float32)
        pieces.append(moved(term.astype(jnp.bfloat16), -1))
    terms.append(tuple(pieces))
    query_grad, total = last_grads(share, start, q, g, stats, kvs, ds_list)
    key_grad, value_grad = sum_terms(total, terms)
    return (query_grad, key_grad, value_grad)


def solution(mesh):
    rows = P(("dp", "ctx"), "tp", None)
    stats = P("tp", "ctx", "dp")
    return jax.shard_map(
        local,
        mesh=mesh,
        in_specs=(rows, rows, rows, rows, stats, stats, P("dp")),
        out_specs=(rows, rows, rows),
        check_vma=False,
    )
```
